256 devices in a mesh: sec: 8 (over x, y_hi), strip: 32 (over z, y_lo, core).
Axes of the slice: x: 4, y: 4 (y_hi: 2, y_lo: 2; y = y_hi * 2 + y_lo), z: 8, core: 2. Of those that a mesh axis runs over, the one named last changes fastest.
Arguments:
- features: bfloat16 [8, 384, 128, 128], P('sec', 'strip'), may hold values from -6 to 6
- offsets: int32 [8], replicated, may hold values from -2 to 2
- state: float32 [2, 8, 384, 128], P(None, 'sec', 'strip'), may hold values from -6 to 6
- w_first: bfloat16 [3, 3, 162, 128], replicated, may hold values from -0.15625 to 0.15625
- b_first: float32 [128], replicated, may hold values from -3 to 3
- w_second: bfloat16 [3, 3, 128, 128], replicated, may hold values from -0.1875 to 0.1875
- b_second: float32 [128], replicated, may hold values from -3 to 3
- w_third: bfloat16 [3, 3, 128, 2], replicated, may hold values from -0.1875 to 0.1875
Outputs:
- updated: float32 [2, 8, 384, 128], P(None, 'sec', 'strip')
The draws below stay inside these ranges and needn't reach their ends.
Inputs may be any that keep to these rules, and one draw needn't show every extreme that they name: offsets[s] is the integer row offset of section s+1 against section s; the last entry is not used.
All inputs are finite; a program needn't handle non-finite values.
Results may differ from the reference program's by a relative error of at most 0.0029.
Values may be sent and summed in bfloat16 or wider, within the bound.
No kernel may reach another device: no remote copies, remote signals or barrier semaphores. Data moves between devices by JAX's collectives and lax.ppermute only.
A program may use at most 64 MiB of HBM per device.

```python
import jax
import jax.numpy as jnp
from jax import lax

C = 128
HID = 128
COLS = 128
SECTIONS = 8
ROWS = 384


def plant(result, key, low, high):
    spot = [jax.random.randint(jax.random.fold_in(key, axis), (), 0, length) for axis, length in enumerate(result.shape)]
    main_axis = result.shape.index(max(result.shape))
    beside = spot[:main_axis] + [(spot[main_axis] + 1) % result.shape[main_axis]] + spot[main_axis + 1:]
    return result.at[tuple(spot)].set(low).at[tuple(beside)].set(high)


def block_levels(key, dims, shards, least, top_value):
    def one(axis_at, blocks):
        heights = jax.random.uniform(jax.random.fold_in(jax.random.fold_in(key, 6), axis_at), (blocks,), jnp.float32, least / len(shards), top_value / len(shards))
        return jnp.repeat(jnp.exp(heights), dims[axis_at] // blocks).reshape((-1,) + (1,) * (len(dims) - axis_at - 1))

    loudness = one(*shards[0])
    for cut in shards[1:]:
        loudness = loudness * one(*cut)
    return loudness


def bell_draw(stream_key, shape, spread, most, split=(), held_as=jnp.bfloat16):
    drawn = spread * jax.random.normal(stream_key, shape, jnp.float32)
    if split:
        drawn = drawn * block_levels(stream_key, shape, split, -0.22, 0.18)
    return jnp.clip(drawn, -most, most).astype(held_as)


def setup_inputs(seed: int = 0) -> dict:
    seeds = jax.random.split(jax.random.key(seed), 9)
    features = bell_draw(seeds[0], (SECTIONS, ROWS, COLS, C), 1.0, 6.0, ((0, 8), (1, 32)))
    offsets = plant(jax.random.randint(seeds[1], (SECTIONS,), -2, 3), jax.random.fold_in(seeds[1], 1), -2, 2).astype(jnp.int32)
    state = bell_draw(seeds[2], (2, SECTIONS, ROWS, COLS), 1.0, 6.0, ((1, 8), (2, 32)), jnp.float32)
    w_first = bell_draw(seeds[3], (3, 3, 162, HID), (9 * 162) ** -0.5, 0.15625)
    b_first = bell_draw(seeds[4], (HID,), 0.5, 3.0, (), jnp.float32)
    w_second = bell_draw(seeds[5], (3, 3, HID, HID), (9 * HID) ** -0.5, 0.1875)
    b_second = bell_draw(seeds[6], (HID,), 0.5, 3.0, (), jnp.float32)
    w_third = bell_draw(seeds[7], (3, 3, HID, 2), (9 * HID) ** -0.5, 0.1875)
    return {"features": features, "offsets": offsets, "state": state, "w_first": w_first, "b_first": b_first, "w_second": w_second, "b_second": b_second, "w_third": w_third}


def corr_pair(mine, other, shift):
    padded = jnp.pad(other.astype(jnp.float32), ((6, 6), (4, 4), (0, 0)))
    mine_f = mine.astype(jnp.float32)
    planes = []
    for row_step in range(-4, 5):
        start = (6 + row_step + shift).astype(jnp.int32)
        taken = lax.dynamic_slice_in_dim(padded, start, ROWS, 0)
        for col_step in range(-4, 5):
            planes.append(jnp.sum(mine_f * taken[:, 4 + col_step:4 + col_step + COLS], axis=-1))
    return jnp.stack(planes)


def convolve(values, kernel, layout):
    return lax.conv_general_dilated(values[None], kernel, (1, 1), ((1, 1), (1, 1)),
                                    dimension_numbers=(layout, "HWIO", "NHWC"),
                                    preferred_element_type=jnp.float32)[0]


def reference(features, offsets, state, w_first, b_first, w_second, b_second, w_third):
    empty = jnp.zeros_like(features[:1])
    below_all = jnp.concatenate([empty, features[:-1]], 0)
    above_all = jnp.concatenate([features[1:], empty], 0)
    shift_above = offsets.astype(jnp.int32)
    shift_below = jnp.concatenate([jnp.zeros((1,), jnp.int32), -offsets[:-1].astype(jnp.int32)], 0)

    def one_section(items):
        mine, below, above, down_shift, up_shift = items
        corr = jnp.concatenate([corr_pair(mine, below, down_shift), corr_pair(mine, above, up_shift)], 0)
        corr = (corr * (C ** -0.5)).astype(jnp.bfloat16)
        hidden_one = jax.nn.relu(convolve(corr, w_first, "NCHW") + b_first).astype(jnp.bfloat16)
        hidden_two = jax.nn.relu(convolve(hidden_one, w_second, "NHWC") + b_second).astype(jnp.bfloat16)
        delta = convolve(hidden_two, w_third, "NHWC")
        return jnp.moveaxis(delta, 2, 0)

    deltas = lax.map(one_section, (features, below_all, above_all, shift_below, shift_above))
    return state + jnp.moveaxis(deltas, 1, 0)
```

```python
import jax
import jax.numpy as jnp
from jax import lax
from jax.experimental import pallas as pl
from jax.experimental.pallas import tpu as pltpu
from jax.sharding import PartitionSpec as P

C = 128
STRIP = 12
HALO = 9
LANES = 128


def corr_rows(src_ref, own_ref, corr_ref, nrot_ref, acc_ref, acc8_ref, base, shift, half):
    for k in range(26):
        turn = 16 * (k % 8)
        row = src_ref[base + (k - 7) + shift]
        if turn:
            nrot_ref[k, turn:] = row[: LANES - turn]
            nrot_ref[k, :turn] = row[LANES - turn :]
        else:
            nrot_ref[k] = row
    col = lax.broadcasted_iota(jnp.int32, (LANES, LANES), 0)
    lane = lax.broadcasted_iota(jnp.int32, (LANES, LANES), 1)
    place = (lane - col + 4) & 127
    for k in range(0, 26, 2):
        first, last = max(0, k - 8), min(17, k + 1)
        right = nrot_ref[k : k + 2].reshape(2 * LANES, C)
        for i in range(first, last + 1):
            both = lax.dot_general(
                own_ref[i], right, (((1,), (1,)), ((), ())), preferred_element_type=jnp.float32
            )
            for side in range(2):
                a = k + side - i
                part = both[:, side * LANES : (side + 1) * LANES]
                if a == 8:
                    acc8_ref[i] = part
                elif 0 <= a < 8:
                    mask = (place >> 4) == (k + side) % 8
                    pltpu.store(acc_ref.at[i], part, mask=mask)
    step_row = (lane * 57) >> 9
    step_col = lane - 9 * step_row
    reach = col + step_col - 4
    valid = (lane < 81) & (reach >= 0) & (reach < LANES)
    start = 16 * step_row + reach
    for i in range(18):
        index = (start + 16 * i) & 127
        merged = jnp.take_along_axis(acc_ref[i], index, axis=1)
        last_a = jnp.take_along_axis(acc8_ref[i], index, axis=1)
        band = jnp.where(lane < 72, merged, last_a) * (C ** (-0.5))
        corr_ref[i, :, half * LANES : (half + 1) * LANES] = jnp.where(valid, band, 0.0).astype(
            jnp.bfloat16
        )


def shifted_sum(wide, bias):
    col = lax.broadcasted_iota(jnp.int32, (LANES, C), 0)
    left = jnp.where(col == 0, 0.0, pltpu.roll(wide[:, :C], 1, 0))
    right = jnp.where(col == LANES - 1, 0.0, pltpu.roll(wide[:, 2 * C :], LANES - 1, 0))
    return left + wide[:, C : 2 * C] + right + bias


def make_kernel(total_rows):
    def kernel(
        scal_ref, own, own_x, own_c, pair, pair_x, pair_c, outer, outer_x, outer_c,
        w1_ref, w2_ref, w3_ref, b1_ref, b2_ref, state_ref, out_ref,
        own_buf, src_buf, nrot_ref, acc_ref, acc8_ref, corr_ref, h1_ref, h2_ref, sems,
    ):
        core = scal_ref[2]
        parity = scal_ref[3]
        top = scal_ref[4]
        copies = [
            (own.at[0], own_buf.at[pl.ds(3, 12)]),
            (own_x.at[0], own_buf.at[pl.ds(15 * core, 3)]),
            (own_c.at[0, pl.ds(9 * core, 3)], own_buf.at[pl.ds(15 * (1 - core), 3)]),
        ]
        for n, (mid, far, near) in enumerate(((pair, pair_x, pair_c), (outer, outer_x, outer_c))):
            copies += [
                (mid.at[0], src_buf.at[n, pl.ds(9 + 3 * core, 12)]),
                (far.at[0], src_buf.at[n, pl.ds(24 * core, 9)]),
                (near.at[0], src_buf.at[n, pl.ds(21 * (1 - core), 12)]),
            ]
        started = [
            pltpu.make_async_copy(src, dst, sems.at[n]) for n, (src, dst) in enumerate(copies)
        ]
        for copy in started:
            copy.start()
        for copy in started:
            copy.wait()
        base = 9 + 3 * core
        corr_rows(
            src_buf.at[1 - parity], own_buf, corr_ref, nrot_ref, acc_ref, acc8_ref, base, scal_ref[0], 0
        )
        corr_rows(
            src_buf.at[parity], own_buf, corr_ref, nrot_ref, acc_ref, acc8_ref, base, scal_ref[1], 1
        )
        for m in range(16):
            left = jnp.concatenate([corr_ref[m], corr_ref[m + 1], corr_ref[m + 2]], axis=1)
            wide = jnp.dot(left, w1_ref[...], preferred_element_type=jnp.float32)
            value = jnp.maximum(shifted_sum(wide, b1_ref[...]), 0.0)
            if m < 2 or m > 13:
                row = top + (m - 2)
                value = jnp.where((row >= 0) & (row < total_rows), value, 0.0)
            h1_ref[m] = value.astype(jnp.bfloat16)
        for n in range(14):
            left = jnp.concatenate([h1_ref[n], h1_ref[n + 1], h1_ref[n + 2]], axis=1)
            wide = jnp.dot(left, w2_ref[...], preferred_element_type=jnp.float32)
            value = jnp.maximum(shifted_sum(wide, b2_ref[...]), 0.0)
            if n < 1 or n > 12:
                row = top + (n - 1)
                value = jnp.where((row >= 0) & (row < total_rows), value, 0.0)
            h2_ref[n] = value.astype(jnp.bfloat16)
        lane = lax.broadcasted_iota(jnp.int32, (8, LANES), 1)
        sums = []
        for n in range(14):
            taps = lax.dot_general(
                w3_ref[...], h2_ref[n], (((1,), (1,)), ((), ())), preferred_element_type=jnp.float32
            )
            left = jnp.where(lane == 0, 0.0, pltpu.roll(taps[:8], 1, 1))
            right = jnp.where(lane == LANES - 1, 0.0, pltpu.roll(taps[16:], LANES - 1, 1))
            sums.append(left + taps[8:16] + right)
        for r in range(12):
            delta = sums[r][0:2] + sums[r + 1][2:4] + sums[r + 2][4:6]
            out_ref[:, 0, r, :] = state_ref[:, 0, r, :] + delta

    return kernel


def align(scal, blocks, weights, biases, state, total_rows):
    hbm = pl.BlockSpec(memory_space=pl.ANY)
    vmem = pl.BlockSpec(memory_space=pltpu.VMEM)
    return pl.pallas_call(
        make_kernel(total_rows),
        out_shape=jax.ShapeDtypeStruct((2, 1, STRIP, LANES), jnp.float32),
        in_specs=[pl.BlockSpec(memory_space=pltpu.SMEM)] + [hbm] * 9 + [vmem] * 6,
        out_specs=vmem,
        scratch_shapes=[
            pltpu.VMEM((18, LANES, C), jnp.bfloat16),
            pltpu.VMEM((2, 33, LANES, C), jnp.bfloat16),
            pltpu.VMEM((26, LANES, C), jnp.bfloat16),
            pltpu.VMEM((18, LANES, LANES), jnp.float32),
            pltpu.VMEM((18, LANES, LANES), jnp.float32),
            pltpu.VMEM((18, LANES, 2 * LANES), jnp.bfloat16),
            pltpu.VMEM((16, LANES, C), jnp.bfloat16),
            pltpu.VMEM((14, LANES, C), jnp.bfloat16),
            pltpu.SemaphoreType.DMA((9,)),
        ],
        compiler_params=pltpu.CompilerParams(vmem_limit_bytes=40 * 1024 * 1024),
    )(scal, *blocks, *weights, *biases, state)


def arranged(w_first, w_second, w_third):
    first = jnp.pad(w_first.reshape(3, 3, 2, 81, 128), ((0, 0), (0, 0), (0, 0), (0, 47), (0, 0)))
    first = first.transpose(0, 2, 3, 1, 4).reshape(768, 384)
    second = w_second.transpose(0, 2, 1, 3).reshape(384, 384)
    third = jnp.pad(w_third.transpose(1, 0, 3, 2).reshape(3, 6, 128), ((0, 0), (0, 2), (0, 0)))
    return first, second, third.reshape(24, 128)


def make_body(sections, strips):
    both = ("sec", "strip")
    core_swap = [(t, t ^ 1) for t in range(strips)]
    chip_swap = [(t, ((t + 1) ^ 1) - 1) for t in range(1, strips - 1)]
    pair_swap = [(s, s ^ 1) for s in range(sections)]
    onward = [(s, s + 2 if s % 2 == 0 else s - 2) for s in range(sections)]
    onward = [(s, d) for s, d in onward if 0 <= d < sections]
    onward_chip = [(s * strips + t, d * strips + u) for s, d in onward for t, u in chip_swap]

    def body(features, offsets, state, w_first, b_first, w_second, b_second, w_third):
        sec = lax.axis_index("sec")
        strip = lax.axis_index("strip")
        core = strip % 2
        shift_above = offsets[sec]
        shift_below = jnp.where(sec > 0, -offsets[jnp.maximum(sec - 1, 0)], 0)
        scal = jnp.stack([shift_below, shift_above, core, sec % 2, strip * STRIP]).astype(jnp.int32)
        pair = lax.ppermute(features, "sec", pair_swap)
        own_x = lax.ppermute(
            lax.dynamic_slice_in_dim(features, 9 * core, 3, 1), "strip", chip_swap
        )
        own_c = lax.ppermute(features, "strip", core_swap)
        outer = lax.ppermute(pair, "sec", onward)
        edge = lax.dynamic_slice_in_dim(pair, 3 * core, HALO, 1)
        outer_x = lax.ppermute(edge, both, onward_chip)
        pair_x = lax.ppermute(edge, "strip", chip_swap)
        pair_c = lax.ppermute(pair, "strip", core_swap)
        outer_c = lax.ppermute(outer, "strip", core_swap)
        return align(
            scal,
            (features, own_x, own_c, pair, pair_x, pair_c, outer, outer_x, outer_c),
            arranged(w_first, w_second, w_third),
            (b_first[None], b_second[None]),
            state,
            strips * STRIP,
        )

    return body


def solution(mesh):
    sections, strips = mesh.shape["sec"], mesh.shape["strip"]
    in_specs = (
        P("sec", "strip", None, None),
        P(),
        P(None, "sec", "strip", None),
        P(),
        P(),
        P(),
        P(),
        P(),
    )
    out_specs = P(None, "sec", "strip", None)
    return jax.shard_map(
        make_body(sections, strips), mesh=mesh, in_specs=in_specs, out_specs=out_specs, check_vma=False
    )
```

```python
import jax
import jax.numpy as jnp
from jax import lax
from jax.experimental import pallas as pl
from jax.experimental.pallas import tpu as pltpu
from jax.sharding import PartitionSpec as P

C = 128
STRIP = 12
HALO = 9
LANES = 128


def corr_rows(src_ref, own_ref, corr_ref, nrot_ref, acc_ref, acc8_ref, base, shift):
    for k in range(26):
        turn = 16 * (k % 8)
        row = src_ref[base + (k - 7) + shift]
        if turn:
            nrot_ref[k, turn:] = row[: LANES - turn]
            nrot_ref[k, :turn] = row[LANES - turn :]
        else:
            nrot_ref[k] = row
    col = lax.broadcasted_iota(jnp.int32, (LANES, LANES), 0)
    lane = lax.broadcasted_iota(jnp.int32, (LANES, LANES), 1)
    place = (lane - col + 4) & 127
    for k in range(0, 26, 2):
        first, last = max(0, k - 8), min(17, k + 1)
        right = nrot_ref[k : k + 2].reshape(2 * LANES, C)
        for i in range(first, last + 1):
            both = lax.dot_general(
                own_ref[i], right, (((1,), (1,)), ((), ())), preferred_element_type=jnp.float32
            )
            for side in range(2):
                a = k + side - i
                part = both[:, side * LANES : (side + 1) * LANES]
                if a == 8:
                    acc8_ref[i] = part
                elif 0 <= a < 8:
                    mask = (place >> 4) == (k + side) % 8
                    pltpu.store(acc_ref.at[i], part, mask=mask)
    step_row = (lane * 57) >> 9
    step_col = lane - 9 * step_row
    reach = col + step_col - 4
    valid = (lane < 81) & (reach >= 0) & (reach < LANES)
    start = 16 * step_row + reach
    for i in range(18):
        index = (start + 16 * i) & 127
        merged = jnp.take_along_axis(acc_ref[i], index, axis=1)
        last_a = jnp.take_along_axis(acc8_ref[i], index, axis=1)
        band = jnp.where(lane < 72, merged, last_a) * (C ** (-0.5))
        corr_ref[i] = jnp.where(valid, band, 0.0).astype(jnp.bfloat16)


def shifted_sum(wide, bias):
    col = lax.broadcasted_iota(jnp.int32, (LANES, C), 0)
    left = jnp.where(col == 0, 0.0, pltpu.roll(wide[:, :C], 1, 0))
    right = jnp.where(col == LANES - 1, 0.0, pltpu.roll(wide[:, 2 * C :], LANES - 1, 0))
    return left + wide[:, C : 2 * C] + right + bias


def position(off_ref):
    sec = lax.axis_index("sec")
    strip = lax.axis_index("strip")
    core = lax.rem(strip, 2)
    parity = lax.rem(sec, 2)
    above = off_ref[sec]
    below = jnp.where(sec > 0, -off_ref[jnp.maximum(sec - 1, 0)], 0)
    return core, parity, strip * STRIP, above, below


def fetched(copies, sems):
    started = [pltpu.make_async_copy(src, dst, sems.at[n]) for n, (src, dst) in enumerate(copies)]
    for copy in started:
        copy.start()
    for copy in started:
        copy.wait()


def stacked(mid, far, near, buf, core, skip):
    whole = near.shape[1] == STRIP
    place = 21 * (1 - core) if whole else 21 - 18 * core
    return [
        (mid.at[0], buf.at[pl.ds(9 + 3 * core, STRIP)]),
        (far.at[0, pl.ds(skip, HALO)], buf.at[pl.ds(24 * core, HALO)]),
        (near.at[0], buf.at[pl.ds(place, near.shape[1])]),
    ]


def pair_kernel(
    off_ref, own, far, own_c, pair, pair_c, w_ref, corr_ref, own_buf, w1_ref,
    src_buf, nrot_ref, acc_ref, acc8_ref, sems,
):
    zeros = jnp.zeros((LANES, C), jnp.bfloat16)
    for dy in range(3):
        for dx in range(3):
            for half in range(2):
                w1_ref[dy, dx, half] = zeros
                w1_ref[dy, dx, half, :81] = w_ref[dy, dx, 81 * half : 81 * half + 81]
    core, parity, top, above, below = position(off_ref)
    copies = [
        (own.at[0], own_buf.at[pl.ds(3, 12)]),
        (far.at[0, pl.ds(0, 3)], own_buf.at[pl.ds(15 * core, 3)]),
        (own_c.at[0, pl.ds(9 * core, 3)], own_buf.at[pl.ds(15 * (1 - core), 3)]),
    ]
    fetched(copies + stacked(pair, far.at[:, pl.ds(3, HALO)], pair_c, src_buf, core, 0), sems)
    shift = jnp.where(parity == 0, above, below)
    corr_rows(src_buf, own_buf, corr_ref, nrot_ref, acc_ref, acc8_ref, 9 + 3 * core, shift)


def make_kernel(total_rows):
    def kernel(
        off_ref, own_buf, pair_corr, outer, outer_x, outer_c,
        w1_ref, w2_ref, w3_ref, b1_ref, b2_ref, state_ref, out_ref,
        src_buf, nrot_ref, acc_ref, acc8_ref, corr_ref, h1_ref, h2_ref, held_ref, sems,
    ):
        core, parity, top, above, below = position(off_ref)
        copies = [(pair_corr, corr_ref.at[1 - parity]), (state_ref, held_ref)]
        fetched(copies + stacked(outer, outer_x, outer_c, src_buf, core, 1 - core), sems)
        shift = jnp.where(parity == 0, below, above)
        corr_rows(
            src_buf, own_buf, corr_ref.at[parity], nrot_ref, acc_ref, acc8_ref, 9 + 3 * core, shift
        )
        first = jnp.concatenate(
            [
                jnp.concatenate([w1_ref[dy, dx, half] for dx in range(3)], axis=1)
                for dy in range(3)
                for half in range(2)
            ],
            axis=0,
        )
        second = jnp.concatenate(
            [jnp.concatenate([w2_ref[dy, dx] for dx in range(3)], axis=1) for dy in range(3)], axis=0
        )
        for m in range(16):
            left = jnp.concatenate(
                [corr_ref[half, m + dy] for dy in range(3) for half in range(2)], axis=1
            )
            wide = jnp.dot(left, first, preferred_element_type=jnp.float32)
            value = jnp.maximum(shifted_sum(wide, b1_ref[...]), 0.0)
            if m < 2 or m > 13:
                row = top + (m - 2)
                value = jnp.where((row >= 0) & (row < total_rows), value, 0.0)
            h1_ref[m] = value.astype(jnp.bfloat16)
        for n in range(14):
            left = jnp.concatenate([h1_ref[n], h1_ref[n + 1], h1_ref[n + 2]], axis=1)
            wide = jnp.dot(left, second, preferred_element_type=jnp.float32)
            value = jnp.maximum(shifted_sum(wide, b2_ref[...]), 0.0)
            if n < 1 or n > 12:
                row = top + (n - 1)
                value = jnp.where((row >= 0) & (row < total_rows), value, 0.0)
            h2_ref[n] = value.astype(jnp.bfloat16)
        lane = lax.broadcasted_iota(jnp.int32, (8, LANES), 1)
        sums = []
        for n in range(14):
            taps = lax.dot_general(
                w3_ref[...], h2_ref[n], (((1,), (1,)), ((), ())), preferred_element_type=jnp.float32
            )
            left = jnp.where(lane == 0, 0.0, pltpu.roll(taps[:8], 1, 1))
            right = jnp.where(lane == LANES - 1, 0.0, pltpu.roll(taps[16:], LANES - 1, 1))
            sums.append(left + taps[8:16] + right)
        for r in range(12):
            delta = sums[r][0:2] + sums[r + 1][2:4] + sums[r + 2][4:6]
            out_ref[:, r, 0, :] = held_ref[:, r, 0, :] + delta

    return kernel


HBM = pl.BlockSpec(memory_space=pl.ANY)
VMEM = pl.BlockSpec(memory_space=pltpu.VMEM)
SMEM = pl.BlockSpec(memory_space=pltpu.SMEM)
PARAMS = pltpu.CompilerParams(vmem_limit_bytes=32 * 1024 * 1024)
SOURCE = [
    pltpu.VMEM((33, LANES, C), jnp.bfloat16),
    pltpu.VMEM((26, LANES, C), jnp.bfloat16),
    pltpu.VMEM((18, LANES, LANES), jnp.float32),
    pltpu.VMEM((18, LANES, LANES), jnp.float32),
]


def pair_corr(offsets, blocks, w_first):
    rows = jax.ShapeDtypeStruct((18, LANES, C), jnp.bfloat16)
    return pl.pallas_call(
        pair_kernel,
        out_shape=(rows, rows, jax.ShapeDtypeStruct((3, 3, 2, LANES, C), jnp.bfloat16)),
        in_specs=[SMEM] + [HBM] * 5 + [VMEM],
        out_specs=(VMEM, VMEM, VMEM),
        scratch_shapes=SOURCE + [pltpu.SemaphoreType.DMA((6,))],
        compiler_params=PARAMS,
        cost_estimate=pl.CostEstimate(
            flops=2 * 18 * 9 * LANES * LANES * C, bytes_accessed=100 * LANES * C * 2, transcendentals=0
        ),
    )(offsets, *blocks, w_first)


def align(offsets, own, blocks, weights, biases, state, total_rows):
    return pl.pallas_call(
        make_kernel(total_rows),
        out_shape=jax.ShapeDtypeStruct((2, STRIP, 1, LANES), jnp.float32),
        in_specs=[SMEM, VMEM] + [HBM] * 4 + [VMEM] * 5 + [HBM],
        out_specs=VMEM,
        scratch_shapes=SOURCE
        + [
            pltpu.VMEM((2, 18, LANES, LANES), jnp.bfloat16),
            pltpu.VMEM((16, LANES, C), jnp.bfloat16),
            pltpu.VMEM((14, LANES, C), jnp.bfloat16),
            pltpu.VMEM((2, STRIP, 1, LANES), jnp.float32),
            pltpu.SemaphoreType.DMA((5,)),
        ],
        compiler_params=PARAMS,
    )(offsets, own, *blocks, *weights, *biases, state)


def arranged(w_third):
    third = jnp.pad(w_third.transpose(1, 0, 3, 2).reshape(3, 6, 128), ((0, 0), (0, 2), (0, 0)))
    return third.reshape(24, 128)


def make_body(sections, strips):
    both = ("sec", "strip")
    core_swap = [(t, t ^ 1) for t in range(strips)]
    chip_swap = [(t, ((t + 1) ^ 1) - 1) for t in range(1, strips - 1)]
    pair_swap = [(s, s ^ 1) for s in range(sections)]
    onward = [(s, s + 2 if s % 2 == 0 else s - 2) for s in range(sections)]
    onward = [(s, d) for s, d in onward if 0 <= d < sections]
    next_chip = [(s ^ 1, d) for s, d in onward]
    next_chip = [(s * strips + t, d * strips + u) for s, d in next_chip for t, u in chip_swap]

    def body(features, offsets, state, w_first, b_first, w_second, b_second, w_third):
        core = lax.rem(lax.axis_index("strip"), 2)
        pair = lax.ppermute(features, "sec", pair_swap)
        own_c = lax.ppermute(features, "strip", core_swap)
        rim = lax.dynamic_slice_in_dim(features, 9 * core, 3, 1)
        edge = lax.dynamic_slice_in_dim(features, 2 * core, HALO + 1, 1)
        third = arranged(w_third)
        pair, own_c, rim, edge, third = lax.optimization_barrier((pair, own_c, rim, edge, third))
        outer = lax.ppermute(pair, "sec", onward)
        far = jnp.concatenate([rim, lax.dynamic_slice_in_dim(pair, 3 * core, HALO, 1)], 1)
        far = lax.ppermute(far, "strip", chip_swap)
        outer_x = lax.ppermute(edge, both, next_chip)
        pair_c = lax.ppermute(pair, "strip", core_swap)
        corr, own_all, first = pair_corr(offsets, (features, far, own_c, pair, pair_c), w_first)
        outer, corr = lax.optimization_barrier((outer, corr))
        near = lax.dynamic_slice_in_dim(outer, 3 * (1 - core), HALO, 1)
        outer_c = lax.ppermute(near, "strip", core_swap)
        out = align(
            offsets,
            own_all,
            (corr, outer, outer_x, outer_c),
            (first, w_second, third),
            (b_first[None], b_second[None]),
            state.reshape(2, STRIP, 1, LANES),
            strips * STRIP,
        )
        return out.reshape(2, 1, STRIP, LANES)

    return body


def solution(mesh):
    sections, strips = mesh.shape["sec"], mesh.shape["strip"]
    in_specs = (
        P("sec", "strip", None, None),
        P(),
        P(None, "sec", "strip", None),
        P(),
        P(),
        P(),
        P(),
        P(),
    )
    out_specs = P(None, "sec", "strip", None)
    return jax.shard_map(
        make_body(sections, strips), mesh=mesh, in_specs=in_specs, out_specs=out_specs, check_vma=False
    )
```

```python
import jax
import jax.numpy as jnp
from jax import lax
from jax.experimental import pallas as pl
from jax.experimental.pallas import tpu as pltpu
from jax.sharding import PartitionSpec as P

C = 128
STRIP = 12
HALO = 9
LANES = 128


def turned(nrot_ref, mid, far, near, core, shift, far_low, far_high, near_low):
    for k in range(26):
        at = k - 7 + shift
        row = mid[0, jnp.clip(at, 0, STRIP - 1)]
        if k < 9:
            low_far = far[0, jnp.clip(at + HALO, 0, HALO - 1) + far_low]
            low_near = near[0, jnp.clip(at + HALO, 0, HALO - 1) + near_low]
            row = jnp.where(at < 0, jnp.where(core == 0, low_far, low_near), row)
        if k > 16:
            high_far = far[0, jnp.clip(at - STRIP, 0, HALO - 1) + far_high]
            high_near = near[0, jnp.clip(at - STRIP, 0, HALO - 1)]
            row = jnp.where(at >= STRIP, jnp.where(core == 0, high_near, high_far), row)
        turn = 16 * (k % 8)
        if turn:
            nrot_ref[k, turn:] = row[: LANES - turn]
            nrot_ref[k, :turn] = row[LANES - turn :]
        else:
            nrot_ref[k] = row


def corr_rows(own_ref, corr_ref, nrot_ref, acc_ref, acc8_ref):
    col = lax.broadcasted_iota(jnp.int32, (LANES, LANES), 0)
    lane = lax.broadcasted_iota(jnp.int32, (LANES, LANES), 1)
    place = (lane - col + 4) & 127
    for k in range(0, 26, 2):
        first, last = max(0, k - 8), min(17, k + 1)
        right = nrot_ref[k : k + 2].reshape(2 * LANES, C)
        for i in range(first, last + 1):
            both = lax.dot_general(
                own_ref[i], right, (((1,), (1,)), ((), ())), preferred_element_type=jnp.float32
            )
            for side in range(2):
                a = k + side - i
                part = both[:, side * LANES : (side + 1) * LANES]
                if a == 8:
                    acc8_ref[i] = part
                elif 0 <= a < 8:
                    mask = (place >> 4) == (k + side) % 8
                    pltpu.store(acc_ref.at[i], part, mask=mask)
    step_row = (lane * 57) >> 9
    step_col = lane - 9 * step_row
    reach = col + step_col - 4
    valid = (lane < 81) & (reach >= 0) & (reach < LANES)
    start = 16 * step_row + reach
    for i in range(18):
        index = (start + 16 * i) & 127
        merged = jnp.take_along_axis(acc_ref[i], index, axis=1)
        last_a = jnp.take_along_axis(acc8_ref[i], index, axis=1)
        band = jnp.where(lane < 72, merged, last_a) * (C ** (-0.5))
        corr_ref[i] = jnp.where(valid, band, 0.0).astype(jnp.bfloat16)


def shifted_sum(wide):
    col = lax.broadcasted_iota(jnp.int32, (LANES, C), 0)
    left = jnp.where(col == 0, 0.0, pltpu.roll(wide[:, :C], 1, 0))
    right = jnp.where(col == LANES - 1, 0.0, pltpu.roll(wide[:, 2 * C :], LANES - 1, 0))
    return left + wide[:, C : 2 * C] + right


def position(off_ref):
    sec = lax.axis_index("sec")
    strip = lax.axis_index("strip")
    core = lax.rem(strip, 2)
    parity = lax.rem(sec, 2)
    above = off_ref[sec]
    below = jnp.where(sec > 0, -off_ref[jnp.maximum(sec - 1, 0)], 0)
    return core, parity, strip * STRIP, above, below


def convolved(rows, kernel_blocks, m):
    left = jnp.concatenate([rows[m + dy] for dy in range(3)], axis=1)
    return jnp.dot(left, kernel_blocks, preferred_element_type=jnp.float32)


def blocks_of(w_ref):
    return jnp.concatenate(
        [jnp.concatenate([w_ref[dy, dx] for dx in range(3)], axis=1) for dy in range(3)], axis=0
    )


def pair_kernel(
    off_ref, own, far, own_c, pair, pair_c, w_ref, b1_ref, b2_ref, part_ref, own_buf, w_outer, b2_out,
    nrot_ref, acc_ref, acc8_ref, corr_ref, w_pair, halves,
):
    core, parity, top, above, below = position(off_ref)
    zeros = jnp.zeros((LANES, C), jnp.bfloat16)
    for dy in range(3):
        for dx in range(3):
            for half in range(2):
                halves[half] = zeros
                halves[half, :81] = w_ref[dy, dx, 81 * half : 81 * half + 81]
            w_pair[dy, dx] = halves[1 - parity]
            w_outer[dy, dx] = halves[parity]
    for r in range(3):
        own_buf[r] = jnp.where(core == 0, far[0, r], own_c[0, 9 + r])
        own_buf[15 + r] = jnp.where(core == 0, own_c[0, r], far[0, r])
    for r in range(STRIP):
        own_buf[3 + r] = own[0, r]
    shift = jnp.where(parity == 0, above, below)
    turned(nrot_ref, pair, far, pair_c, core, shift, 3, 3, 3)
    corr_rows(own_buf, corr_ref, nrot_ref, acc_ref, acc8_ref)
    b2_out[...] = b2_ref[...]
    kernel_blocks = blocks_of(w_pair)
    for m in range(16):
        part_ref[m] = shifted_sum(convolved(corr_ref, kernel_blocks, m)) + b1_ref[...]


def make_kernel(total_rows):
    def kernel(
        off_ref, part_ref, own_buf, outer, outer_x, outer_c, w1_ref, w2_ref, w3_ref, b2_ref,
        state_ref, out_ref, nrot_ref, acc_ref, acc8_ref, corr_ref, h1_ref, h2_ref, held_ref, sem,
    ):
        held = pltpu.make_async_copy(state_ref, held_ref, sem)
        held.start()
        core, parity, top, above, below = position(off_ref)
        shift = jnp.where(parity == 0, below, above)
        turned(nrot_ref, outer, outer_x, outer_c, core, shift, 1, 0, 0)
        corr_rows(own_buf, corr_ref, nrot_ref, acc_ref, acc8_ref)
        first = blocks_of(w1_ref)
        second = blocks_of(w2_ref)
        for m in range(16):
            value = jnp.maximum(part_ref[m] + shifted_sum(convolved(corr_ref, first, m)), 0.0)
            if m < 2 or m > 13:
                row = top + (m - 2)
                value = jnp.where((row >= 0) & (row < total_rows), value, 0.0)
            h1_ref[m] = value.astype(jnp.bfloat16)
        for n in range(14):
            value = jnp.maximum(shifted_sum(convolved(h1_ref, second, n)) + b2_ref[...], 0.0)
            if n < 1 or n > 12:
                row = top + (n - 1)
                value = jnp.where((row >= 0) & (row < total_rows), value, 0.0)
            h2_ref[n] = value.astype(jnp.bfloat16)
        lane = lax.broadcasted_iota(jnp.int32, (8, LANES), 1)
        sums = []
        for n in range(14):
            taps = lax.dot_general(
                w3_ref[...], h2_ref[n], (((1,), (1,)), ((), ())), preferred_element_type=jnp.float32
            )
            left = jnp.where(lane == 0, 0.0, pltpu.roll(taps[:8], 1, 1))
            right = jnp.where(lane == LANES - 1, 0.0, pltpu.roll(taps[16:], LANES - 1, 1))
            sums.append(left + taps[8:16] + right)
        held.wait()
        for r in range(12):
            delta = sums[r][0:2] + sums[r + 1][2:4] + sums[r + 2][4:6]
            out_ref[:, r, 0, :] = held_ref[:, r, 0, :] + delta

    return kernel


HBM = pl.BlockSpec(memory_space=pl.ANY)
VMEM = pl.BlockSpec(memory_space=pltpu.VMEM)
SMEM = pl.BlockSpec(memory_space=pltpu.SMEM)
PARAMS = pltpu.CompilerParams(vmem_limit_bytes=32 * 1024 * 1024)
CORR = [
    pltpu.VMEM((26, LANES, C), jnp.bfloat16),
    pltpu.VMEM((18, LANES, LANES), jnp.float32),
    pltpu.VMEM((18, LANES, LANES), jnp.float32),
    pltpu.VMEM((18, LANES, LANES), jnp.bfloat16),
]
TAPS = pltpu.VMEM((3, 3, LANES, C), jnp.bfloat16)


def pair_part(offsets, blocks, w_first, b_first, b_second):
    return pl.pallas_call(
        pair_kernel,
        out_shape=(
            jax.ShapeDtypeStruct((16, LANES, C), jnp.float32),
            jax.ShapeDtypeStruct((18, LANES, C), jnp.bfloat16),
            jax.ShapeDtypeStruct((3, 3, LANES, C), jnp.bfloat16),
            jax.ShapeDtypeStruct((1, C), jnp.float32),
        ),
        in_specs=[SMEM] + [VMEM] * 8,
        out_specs=(VMEM, VMEM, VMEM, VMEM),
        scratch_shapes=CORR + [TAPS, pltpu.VMEM((2, LANES, C), jnp.bfloat16)],
        compiler_params=PARAMS,
        cost_estimate=pl.CostEstimate(
            flops=2 * 18 * 9 * LANES * LANES * C, bytes_accessed=100 * LANES * C * 2, transcendentals=0
        ),
    )(offsets, *blocks, w_first, b_first, b_second)


def align(offsets, part, own, blocks, weights, b_second, state, total_rows):
    return pl.pallas_call(
        make_kernel(total_rows),
        out_shape=jax.ShapeDtypeStruct((2, STRIP, 1, LANES), jnp.float32),
        in_specs=[SMEM] + [VMEM] * 9 + [HBM],
        out_specs=VMEM,
        scratch_shapes=CORR
        + [
            pltpu.VMEM((16, LANES, C), jnp.bfloat16),
            pltpu.VMEM((14, LANES, C), jnp.bfloat16),
            pltpu.VMEM((2, STRIP, 1, LANES), jnp.float32),
            pltpu.SemaphoreType.DMA,
        ],
        compiler_params=PARAMS,
    )(offsets, part, own, *blocks, *weights, b_second, state)


def arranged(w_third):
    third = jnp.pad(w_third.transpose(1, 0, 3, 2).reshape(3, 6, 128), ((0, 0), (0, 2), (0, 0)))
    return third.reshape(24, 128)


def make_body(sections, strips):
    both = ("sec", "strip")
    core_swap = [(t, t ^ 1) for t in range(strips)]
    chip_swap = [(t, ((t + 1) ^ 1) - 1) for t in range(1, strips - 1)]
    pair_swap = [(s, s ^ 1) for s in range(sections)]
    onward = [(s, s + 2 if s % 2 == 0 else s - 2) for s in range(sections)]
    onward = [(s, d) for s, d in onward if 0 <= d < sections]
    next_chip = [(s ^ 1, d) for s, d in onward]
    next_chip = [(s * strips + t, d * strips + u) for s, d in next_chip for t, u in chip_swap]

    def body(features, offsets, state, w_first, b_first, w_second, b_second, w_third):
        core = lax.rem(lax.axis_index("strip"), 2)
        pair = lax.ppermute(features, "sec", pair_swap)
        own_c = lax.ppermute(features, "strip", core_swap)
        rim = lax.dynamic_slice_in_dim(features, 9 * core, 3, 1)
        edge = lax.dynamic_slice_in_dim(features, 2 * core, HALO + 1, 1)
        third = arranged(w_third)
        pair, own_c, rim, edge, third = lax.optimization_barrier((pair, own_c, rim, edge, third))
        outer = lax.ppermute(pair, "sec", onward)
        far = jnp.concatenate([rim, lax.dynamic_slice_in_dim(pair, 3 * core, HALO, 1)], 1)
        far = lax.ppermute(far, "strip", chip_swap)
        outer_x = lax.ppermute(edge, both, next_chip)
        pair_c = lax.ppermute(pair, "strip", core_swap)
        part, own_all, first, bias = pair_part(
            offsets, (features, far, own_c, pair, pair_c), w_first, b_first[None], b_second[None]
        )
        outer, part = lax.optimization_barrier((outer, part))
        near = lax.dynamic_slice_in_dim(outer, 3 * (1 - core), HALO, 1)
        outer_c = lax.ppermute(near, "strip", core_swap)
        out = align(
            offsets,
            part,
            own_all,
            (outer, outer_x, outer_c),
            (first, w_second, third),
            bias,
            state.reshape(2, STRIP, 1, LANES),
            strips * STRIP,
        )
        return out.reshape(2, 1, STRIP, LANES)

    return body


def solution(mesh):
    sections, strips = mesh.shape["sec"], mesh.shape["strip"]
    in_specs = (
        P("sec", "strip", None, None),
        P(),
        P(None, "sec", "strip", None),
        P(),
        P(),
        P(),
        P(),
        P(),
    )
    out_specs = P(None, "sec", "strip", None)
    return jax.shard_map(
        make_body(sections, strips), mesh=mesh, in_specs=in_specs, out_specs=out_specs, check_vma=False
    )
```

```python
import jax
import jax.numpy as jnp
from jax import lax
from jax.experimental import pallas as pl
from jax.experimental.pallas import tpu as pltpu
from jax.sharding import PartitionSpec as P

C = 128
STRIP = 12
HALO = 9
LANES = 128


def turned(nrot_ref, mid, far, near, core, shift, far_low, far_high, near_low):
    for k in range(26):
        at = k - 7 + shift
        row = mid[0, jnp.clip(at, 0, STRIP - 1)]
        if k < 9:
            low_far = far[0, jnp.clip(at + HALO, 0, HALO - 1) + far_low]
            low_near = near[0, jnp.clip(at + HALO, 0, HALO - 1) + near_low]
            row = jnp.where(at < 0, jnp.where(core == 0, low_far, low_near), row)
        if k > 16:
            high_far = far[0, jnp.clip(at - STRIP, 0, HALO - 1) + far_high]
            high_near = near[0, jnp.clip(at - STRIP, 0, HALO - 1)]
            row = jnp.where(at >= STRIP, jnp.where(core == 0, high_near, high_far), row)
        turn = 16 * (k % 8)
        if turn:
            nrot_ref[k, turn:] = row[: LANES - turn]
            nrot_ref[k, :turn] = row[LANES - turn :]
        else:
            nrot_ref[k] = row


def corr_rows(own_ref, corr_ref, nrot_ref, acc_ref, acc8_ref):
    col = lax.broadcasted_iota(jnp.int32, (LANES, LANES), 0)
    lane = lax.broadcasted_iota(jnp.int32, (LANES, LANES), 1)
    place = (lane - col + 4) & 127
    for k in range(0, 26, 2):
        first, last = max(0, k - 8), min(17, k + 1)
        right = nrot_ref[k : k + 2].reshape(2 * LANES, C)
        for i in range(first, last + 1):
            both = lax.dot_general(
                own_ref[i], right, (((1,), (1,)), ((), ())), preferred_element_type=jnp.float32
            )
            for side in range(2):
                a = k + side - i
                part = both[:, side * LANES : (side + 1) * LANES]
                if a == 8:
                    acc8_ref[i] = part
                elif 0 <= a < 8:
                    mask = (place >> 4) == (k + side) % 8
                    pltpu.store(acc_ref.at[i], part, mask=mask)
    step_row = (lane * 57) >> 9
    step_col = lane - 9 * step_row
    reach = col + step_col - 4
    valid = (reach >= 0) & (reach < LANES)
    start = 16 * step_row + reach
    for i in range(18):
        index = (start + 16 * i) & 127
        merged = jnp.take_along_axis(acc_ref[i], index, axis=1)
        last_a = jnp.take_along_axis(acc8_ref[i], index, axis=1)
        band = jnp.where(lane < 72, merged, last_a) * (C ** (-0.5))
        head = jnp.where(valid[:8], band[:8], 0.0)
        tail = jnp.where(valid[-8:], band[-8:], 0.0)
        corr_ref[i] = jnp.concatenate([head, band[8:-8], tail], axis=0).astype(jnp.bfloat16)


def shifted_sum(wide):
    row = lax.broadcasted_iota(jnp.int32, (8, C), 0)
    left = pltpu.roll(wide[:, :C], 1, 0)
    left = jnp.concatenate([jnp.where(row == 0, 0.0, left[:8]), left[8:]], axis=0)
    right = pltpu.roll(wide[:, 2 * C :], LANES - 1, 0)
    right = jnp.concatenate([right[:-8], jnp.where(row == 7, 0.0, right[-8:])], axis=0)
    return left + wide[:, C : 2 * C] + right


def position(off_ref):
    sec = lax.axis_index("sec")
    strip = lax.axis_index("strip")
    core = lax.rem(strip, 2)
    parity = lax.rem(sec, 2)
    above = off_ref[sec]
    below = jnp.where(sec > 0, -off_ref[jnp.maximum(sec - 1, 0)], 0)
    return core, parity, strip * STRIP, above, below


def convolved(rows, kernel_blocks, m):
    left = jnp.concatenate([rows[m + dy] for dy in range(4)], axis=1)
    both = jnp.dot(left, kernel_blocks, preferred_element_type=jnp.float32)
    return shifted_sum(both[:, : 3 * C]), shifted_sum(both[:, 3 * C :])


def blocks_of(w_ref):
    zeros = jnp.zeros((C, 3 * C), jnp.bfloat16)
    taps = [jnp.concatenate([w_ref[dy, dx] for dx in range(3)], axis=1) for dy in range(3)]
    low = jnp.concatenate(taps + [zeros], axis=0)
    return jnp.concatenate([low, jnp.concatenate([zeros] + taps, axis=0)], axis=1)


def pair_kernel(
    off_ref, own, far, own_c, pair, pair_c, w_ref, b1_ref, b2_ref, part_ref, own_buf, w_outer, b2_out,
    nrot_ref, acc_ref, acc8_ref, corr_ref, w_pair, halves,
):
    core, parity, top, above, below = position(off_ref)
    zeros = jnp.zeros((LANES, C), jnp.bfloat16)
    for dy in range(3):
        for dx in range(3):
            for half in range(2):
                halves[half] = zeros
                halves[half, :81] = w_ref[dy, dx, 81 * half : 81 * half + 81]
            w_pair[dy, dx] = halves[1 - parity]
            w_outer[dy, dx] = halves[parity]
    for r in range(3):
        own_buf[r] = jnp.where(core == 0, far[0, r], own_c[0, 9 + r])
        own_buf[15 + r] = jnp.where(core == 0, own_c[0, r], far[0, r])
    for r in range(STRIP):
        own_buf[3 + r] = own[0, r]
    shift = jnp.where(parity == 0, above, below)
    turned(nrot_ref, pair, far, pair_c, core, shift, 3, 3, 3)
    corr_rows(own_buf, corr_ref, nrot_ref, acc_ref, acc8_ref)
    b2_out[...] = b2_ref[...]
    kernel_blocks = blocks_of(w_pair)
    for m in range(0, 16, 2):
        for side, value in enumerate(convolved(corr_ref, kernel_blocks, m)):
            part_ref[m + side] = value + b1_ref[...]


def make_kernel(total_rows):
    def kernel(
        off_ref, part_ref, own_buf, outer, outer_x, outer_c, w1_ref, w2_ref, w3_ref, b2_ref,
        state_ref, out_ref, nrot_ref, acc_ref, acc8_ref, corr_ref, h1_ref, h2_ref, held_ref, sem,
    ):
        held = pltpu.make_async_copy(state_ref, held_ref, sem)
        held.start()
        core, parity, top, above, below = position(off_ref)
        shift = jnp.where(parity == 0, below, above)
        turned(nrot_ref, outer, outer_x, outer_c, core, shift, 1, 0, 0)
        corr_rows(own_buf, corr_ref, nrot_ref, acc_ref, acc8_ref)
        first = blocks_of(w1_ref)
        second = blocks_of(w2_ref)
        for m in range(0, 16, 2):
            for r, value in enumerate(convolved(corr_ref, first, m), m):
                value = jnp.maximum(part_ref[r] + value, 0.0)
                if r < 2 or r > 13:
                    row = top + (r - 2)
                    value = jnp.where((row >= 0) & (row < total_rows), value, 0.0)
                h1_ref[r] = value.astype(jnp.bfloat16)
        for n in range(0, 14, 2):
            for r, value in enumerate(convolved(h1_ref, second, n), n):
                value = jnp.maximum(value + b2_ref[...], 0.0)
                if r < 1 or r > 12:
                    row = top + (r - 1)
                    value = jnp.where((row >= 0) & (row < total_rows), value, 0.0)
                h2_ref[r] = value.astype(jnp.bfloat16)
        lane = lax.broadcasted_iota(jnp.int32, (8, LANES), 1)
        sums = []
        for n in range(0, 14, 2):
            taps = lax.dot_general(
                w3_ref[...],
                h2_ref[n : n + 2].reshape(2 * LANES, C),
                (((1,), (1,)), ((), ())),
                preferred_element_type=jnp.float32,
            )
            for side in range(2):
                tap = taps[:, side * LANES : (side + 1) * LANES]
                left = jnp.where(lane == 0, 0.0, pltpu.roll(tap[:8], 1, 1))
                right = jnp.where(lane == LANES - 1, 0.0, pltpu.roll(tap[16:], LANES - 1, 1))
                sums.append(left + tap[8:16] + right)
        held.wait()
        for r in range(12):
            delta = sums[r][0:2] + sums[r + 1][2:4] + sums[r + 2][4:6]
            out_ref[:, r, 0, :] = held_ref[:, r, 0, :] + delta

    return kernel


HBM = pl.BlockSpec(memory_space=pl.ANY)
VMEM = pl.BlockSpec(memory_space=pltpu.VMEM)
SMEM = pl.BlockSpec(memory_space=pltpu.SMEM)
PARAMS = pltpu.CompilerParams(vmem_limit_bytes=32 * 1024 * 1024)
CORR = [
    pltpu.VMEM((26, LANES, C), jnp.bfloat16),
    pltpu.VMEM((18, LANES, LANES), jnp.float32),
    pltpu.VMEM((18, LANES, LANES), jnp.float32),
    pltpu.VMEM((18, LANES, LANES), jnp.bfloat16),
]
TAPS = pltpu.VMEM((3, 3, LANES, C), jnp.bfloat16)


def pair_part(offsets, blocks, w_first, b_first, b_second):
    return pl.pallas_call(
        pair_kernel,
        out_shape=(
            jax.ShapeDtypeStruct((16, LANES, C), jnp.float32),
            jax.ShapeDtypeStruct((18, LANES, C), jnp.bfloat16),
            jax.ShapeDtypeStruct((3, 3, LANES, C), jnp.bfloat16),
            jax.ShapeDtypeStruct((1, C), jnp.float32),
        ),
        in_specs=[SMEM] + [VMEM] * 8,
        out_specs=(VMEM, VMEM, VMEM, VMEM),
        scratch_shapes=CORR + [TAPS, pltpu.VMEM((2, LANES, C), jnp.bfloat16)],
        compiler_params=PARAMS,
        cost_estimate=pl.CostEstimate(
            flops=2 * 18 * 9 * LANES * LANES * C, bytes_accessed=100 * LANES * C * 2, transcendentals=0
        ),
    )(offsets, *blocks, w_first, b_first, b_second)


def align(offsets, part, own, blocks, weights, b_second, state, total_rows):
    return pl.pallas_call(
        make_kernel(total_rows),
        out_shape=jax.ShapeDtypeStruct((2, STRIP, 1, LANES), jnp.float32),
        in_specs=[SMEM] + [VMEM] * 9 + [HBM],
        out_specs=VMEM,
        scratch_shapes=CORR
        + [
            pltpu.VMEM((16, LANES, C), jnp.bfloat16),
            pltpu.VMEM((14, LANES, C), jnp.bfloat16),
            pltpu.VMEM((2, STRIP, 1, LANES), jnp.float32),
            pltpu.SemaphoreType.DMA,
        ],
        compiler_params=PARAMS,
    )(offsets, part, own, *blocks, *weights, b_second, state)


def arranged(w_third):
    third = jnp.pad(w_third.transpose(1, 0, 3, 2).reshape(3, 6, 128), ((0, 0), (0, 2), (0, 0)))
    return third.reshape(24, 128)


def make_body(sections, strips):
    both = ("sec", "strip")
    core_swap = [(t, t ^ 1) for t in range(strips)]
    chip_swap = [(t, ((t + 1) ^ 1) - 1) for t in range(1, strips - 1)]
    pair_swap = [(s, s ^ 1) for s in range(sections)]
    onward = [(s, s + 2 if s % 2 == 0 else s - 2) for s in range(sections)]
    onward = [(s, d) for s, d in onward if 0 <= d < sections]
    next_chip = [(s ^ 1, d) for s, d in onward]
    next_chip = [(s * strips + t, d * strips + u) for s, d in next_chip for t, u in chip_swap]

    def body(features, offsets, state, w_first, b_first, w_second, b_second, w_third):
        core = lax.rem(lax.axis_index("strip"), 2)
        pair = lax.ppermute(features, "sec", pair_swap)
        own_c = lax.ppermute(features, "strip", core_swap)
        rim = lax.dynamic_slice_in_dim(features, 9 * core, 3, 1)
        edge = lax.dynamic_slice_in_dim(features, 2 * core, HALO + 1, 1)
        third = arranged(w_third)
        pair, own_c, rim, edge, third = lax.optimization_barrier((pair, own_c, rim, edge, third))
        outer = lax.ppermute(pair, "sec", onward)
        far = jnp.concatenate([rim, lax.dynamic_slice_in_dim(pair, 3 * core, HALO, 1)], 1)
        far = lax.ppermute(far, "strip", chip_swap)
        outer_x = lax.ppermute(edge, both, next_chip)
        pair_c = lax.ppermute(pair, "strip", core_swap)
        part, own_all, first, bias = pair_part(
            offsets, (features, far, own_c, pair, pair_c), w_first, b_first[None], b_second[None]
        )
        outer, part = lax.optimization_barrier((outer, part))
        near = lax.dynamic_slice_in_dim(outer, 3 * (1 - core), HALO, 1)
        outer_c = lax.ppermute(near, "strip", core_swap)
        out = align(
            offsets,
            part,
            own_all,
            (outer, outer_x, outer_c),
            (first, w_second, third),
            bias,
            state.reshape(2, STRIP, 1, LANES),
            strips * STRIP,
        )
        return out.reshape(2, 1, STRIP, LANES)

    return body


def solution(mesh):
    sections, strips = mesh.shape["sec"], mesh.shape["strip"]
    in_specs = (
        P("sec", "strip", None, None),
        P(),
        P(None, "sec", "strip", None),
        P(),
        P(),
        P(),
        P(),
        P(),
    )
    out_specs = P(None, "sec", "strip", None)
    return jax.shard_map(
        make_body(sections, strips), mesh=mesh, in_specs=in_specs, out_specs=out_specs, check_vma=False
    )
```

```python
import jax
import jax.numpy as jnp
from jax import lax
from jax.experimental import pallas as pl
from jax.experimental.pallas import tpu as pltpu
from jax.sharding import PartitionSpec as P

C = 128
STRIP = 12
HALO = 9
LANES = 128


def turned(nrot_ref, mid, far, near, core, shift, far_low, far_high, near_low):
    for k in range(26):
        at = k - 7 + shift
        row = mid[0, jnp.clip(at, 0, STRIP - 1)]
        if k < 9:
            low_far = far[0, jnp.clip(at + HALO, 0, HALO - 1) + far_low]
            low_near = near[0, jnp.clip(at + HALO, 0, HALO - 1) + near_low]
            row = jnp.where(at < 0, jnp.where(core == 0, low_far, low_near), row)
        if k > 16:
            high_far = far[0, jnp.clip(at - STRIP, 0, HALO - 1) + far_high]
            high_near = near[0, jnp.clip(at - STRIP, 0, HALO - 1)]
            row = jnp.where(at >= STRIP, jnp.where(core == 0, high_near, high_far), row)
        turn = 16 * (k % 8)
        if turn:
            nrot_ref[k, turn:] = row[: LANES - turn]
            nrot_ref[k, :turn] = row[LANES - turn :]
        else:
            nrot_ref[k] = row


def corr_rows(own_ref, corr_ref, nrot_ref, acc_ref, acc8_ref):
    col = lax.broadcasted_iota(jnp.int32, (LANES, LANES), 0)
    lane = lax.broadcasted_iota(jnp.int32, (LANES, LANES), 1)
    place = (lane - col + 4) & 127
    for k in range(0, 26, 2):
        first, last = max(0, k - 8), min(17, k + 1)
        right = nrot_ref[k : k + 2].reshape(2 * LANES, C)
        for i in range(first, last + 1):
            both = lax.dot_general(
                own_ref[i], right, (((1,), (1,)), ((), ())), preferred_element_type=jnp.float32
            )
            for side in range(2):
                a = k + side - i
                part = both[:, side * LANES : (side + 1) * LANES]
                if a == 8:
                    acc8_ref[i] = part
                elif 0 <= a < 8:
                    mask = (place >> 4) == (k + side) % 8
                    pltpu.store(acc_ref.at[i], part, mask=mask)
    step_row = (lane * 57) >> 9
    step_col = lane - 9 * step_row
    reach = col + step_col - 4
    valid = (reach >= 0) & (reach < LANES)
    start = 16 * step_row + reach
    for i in range(18):
        index = (start + 16 * i) & 127
        merged = jnp.take_along_axis(acc_ref[i], index, axis=1)
        last_a = jnp.take_along_axis(acc8_ref[i], index, axis=1)
        band = jnp.where(lane < 72, merged, last_a) * (C ** (-0.5))
        head = jnp.where(valid[:8], band[:8], 0.0)
        tail = jnp.where(valid[-8:], band[-8:], 0.0)
        corr_ref[i] = jnp.concatenate([head, band[8:-8], tail], axis=0).astype(jnp.bfloat16)


def shifted_sum(wide):
    row = lax.broadcasted_iota(jnp.int32, (8, C), 0)
    left = pltpu.roll(wide[:, :C], 1, 0)
    left = jnp.concatenate([jnp.where(row == 0, 0.0, left[:8]), left[8:]], axis=0)
    right = pltpu.roll(wide[:, 2 * C :], LANES - 1, 0)
    right = jnp.concatenate([right[:-8], jnp.where(row == 7, 0.0, right[-8:])], axis=0)
    return left + wide[:, C : 2 * C] + right


def position(off_ref):
    sec = lax.axis_index("sec")
    strip = lax.axis_index("strip")
    core = lax.rem(strip, 2)
    parity = lax.rem(sec, 2)
    above = off_ref[sec]
    below = jnp.where(sec > 0, -off_ref[jnp.maximum(sec - 1, 0)], 0)
    return core, parity, strip * STRIP, above, below


def convolved(rows, kernel_blocks, m):
    left = jnp.concatenate([rows[m + dy] for dy in range(4)], axis=1)
    both = jnp.dot(left, kernel_blocks, preferred_element_type=jnp.float32)
    return shifted_sum(both[:, : 3 * C]), shifted_sum(both[:, 3 * C :])


def blocks_of(w_ref):
    zeros = jnp.zeros((C, 3 * C), jnp.bfloat16)
    taps = [jnp.concatenate([w_ref[dy, dx] for dx in range(3)], axis=1) for dy in range(3)]
    low = jnp.concatenate(taps + [zeros], axis=0)
    return jnp.concatenate([low, jnp.concatenate([zeros] + taps, axis=0)], axis=1)


def pair_kernel(
    off_ref, own, far, own_c, pair, pair_c, w_ref, b1_ref, b2_ref, part_ref, own_buf, w_outer, b2_out,
    nrot_ref, acc_ref, acc8_ref, corr_ref, w_pair, halves,
):
    core, parity, top, above, below = position(off_ref)
    zeros = jnp.zeros((LANES, C), jnp.bfloat16)
    for dy in range(3):
        for dx in range(3):
            for half in range(2):
                halves[half] = zeros
                halves[half, :81] = w_ref[dy, dx, 81 * half : 81 * half + 81]
            w_pair[dy, dx] = halves[1 - parity]
            w_outer[dy, dx] = halves[parity]
    for r in range(3):
        own_buf[r] = jnp.where(core == 0, far[0, r], own_c[0, 9 + r])
        own_buf[15 + r] = jnp.where(core == 0, own_c[0, r], far[0, r])
    for r in range(STRIP):
        own_buf[3 + r] = own[0, r]
    shift = jnp.where(parity == 0, above, below)
    turned(nrot_ref, pair, far, pair_c, core, shift, 3, 3, 0)
    corr_rows(own_buf, corr_ref, nrot_ref, acc_ref, acc8_ref)
    b2_out[...] = b2_ref[...]
    kernel_blocks = blocks_of(w_pair)
    for m in range(0, 16, 2):
        for side, value in enumerate(convolved(corr_ref, kernel_blocks, m)):
            part_ref[m + side] = value + b1_ref[...]


def make_kernel(total_rows):
    def kernel(
        off_ref, part_ref, own_buf, outer, outer_x, outer_c, w1_ref, w2_ref, w3_ref, b2_ref,
        state_ref, out_ref, nrot_ref, acc_ref, acc8_ref, corr_ref, h1_ref, h2_ref, held_ref, sem,
    ):
        held = pltpu.make_async_copy(state_ref, held_ref, sem)
        held.start()
        core, parity, top, above, below = position(off_ref)
        shift = jnp.where(parity == 0, below, above)
        turned(nrot_ref, outer, outer_x, outer_c, core, shift, 0, 0, 0)
        corr_rows(own_buf, corr_ref, nrot_ref, acc_ref, acc8_ref)
        first = blocks_of(w1_ref)
        second = blocks_of(w2_ref)
        for m in range(0, 16, 2):
            for r, value in enumerate(convolved(corr_ref, first, m), m):
                value = jnp.maximum(part_ref[r] + value, 0.0)
                if r < 2 or r > 13:
                    row = top + (r - 2)
                    value = jnp.where((row >= 0) & (row < total_rows), value, 0.0)
                h1_ref[r] = value.astype(jnp.bfloat16)
        for n in range(0, 14, 2):
            for r, value in enumerate(convolved(h1_ref, second, n), n):
                value = jnp.maximum(value + b2_ref[...], 0.0)
                if r < 1 or r > 12:
                    row = top + (r - 1)
                    value = jnp.where((row >= 0) & (row < total_rows), value, 0.0)
                h2_ref[r] = value.astype(jnp.bfloat16)
        lane = lax.broadcasted_iota(jnp.int32, (8, LANES), 1)
        sums = []
        for n in range(0, 14, 2):
            taps = lax.dot_general(
                w3_ref[...],
                h2_ref[n : n + 2].reshape(2 * LANES, C),
                (((1,), (1,)), ((), ())),
                preferred_element_type=jnp.float32,
            )
            for side in range(2):
                tap = taps[:, side * LANES : (side + 1) * LANES]
                left = jnp.where(lane == 0, 0.0, pltpu.roll(tap[:8], 1, 1))
                right = jnp.where(lane == LANES - 1, 0.0, pltpu.roll(tap[16:], LANES - 1, 1))
                sums.append(left + tap[8:16] + right)
        held.wait()
        for r in range(12):
            delta = sums[r][0:2] + sums[r + 1][2:4] + sums[r + 2][4:6]
            out_ref[:, r, 0, :] = held_ref[:, r, 0, :] + delta

    return kernel


HBM = pl.BlockSpec(memory_space=pl.ANY)
VMEM = pl.BlockSpec(memory_space=pltpu.VMEM)
SMEM = pl.BlockSpec(memory_space=pltpu.SMEM)
PARAMS = pltpu.CompilerParams(vmem_limit_bytes=32 * 1024 * 1024)
CORR = [
    pltpu.VMEM((26, LANES, C), jnp.bfloat16),
    pltpu.VMEM((18, LANES, LANES), jnp.float32),
    pltpu.VMEM((18, LANES, LANES), jnp.float32),
    pltpu.VMEM((18, LANES, LANES), jnp.bfloat16),
]
TAPS = pltpu.VMEM((3, 3, LANES, C), jnp.bfloat16)


def pair_part(offsets, blocks, w_first, b_first, b_second):
    return pl.pallas_call(
        pair_kernel,
        out_shape=(
            jax.ShapeDtypeStruct((16, LANES, C), jnp.float32),
            jax.ShapeDtypeStruct((18, LANES, C), jnp.bfloat16),
            jax.ShapeDtypeStruct((3, 3, LANES, C), jnp.bfloat16),
            jax.ShapeDtypeStruct((1, C), jnp.float32),
        ),
        in_specs=[SMEM] + [VMEM] * 8,
        out_specs=(VMEM, VMEM, VMEM, VMEM),
        scratch_shapes=CORR + [TAPS, pltpu.VMEM((2, LANES, C), jnp.bfloat16)],
        compiler_params=PARAMS,
        cost_estimate=pl.CostEstimate(
            flops=2 * 18 * 9 * LANES * LANES * C, bytes_accessed=100 * LANES * C * 2, transcendentals=0
        ),
    )(offsets, *blocks, w_first, b_first, b_second)


def align(offsets, part, own, blocks, weights, b_second, state, total_rows):
    return pl.pallas_call(
        make_kernel(total_rows),
        out_shape=jax.ShapeDtypeStruct((2, STRIP, 1, LANES), jnp.float32),
        in_specs=[SMEM] + [VMEM] * 9 + [HBM],
        out_specs=VMEM,
        scratch_shapes=CORR
        + [
            pltpu.VMEM((16, LANES, C), jnp.bfloat16),
            pltpu.VMEM((14, LANES, C), jnp.bfloat16),
            pltpu.VMEM((2, STRIP, 1, LANES), jnp.float32),
            pltpu.SemaphoreType.DMA,
        ],
        compiler_params=PARAMS,
    )(offsets, part, own, *blocks, *weights, b_second, state)


def arranged(w_third):
    third = jnp.pad(w_third.transpose(1, 0, 3, 2).reshape(3, 6, 128), ((0, 0), (0, 2), (0, 0)))
    return third.reshape(24, 128)


def make_body(sections, strips):
    both = ("sec", "strip")
    core_swap = [(t, t ^ 1) for t in range(strips)]
    chip_swap = [(t, ((t + 1) ^ 1) - 1) for t in range(1, strips - 1)]
    pair_swap = [(s, s ^ 1) for s in range(sections)]
    onward = [(s, s + 2 if s % 2 == 0 else s - 2) for s in range(sections)]
    onward = [(s, d) for s, d in onward if 0 <= d < sections]
    next_chip = [(s ^ 1, d) for s, d in onward]
    next_chip = [(s * strips + t, d * strips + u) for s, d in next_chip for t, u in chip_swap]

    def body(features, offsets, state, w_first, b_first, w_second, b_second, w_third):
        core = lax.rem(lax.axis_index("strip"), 2)
        pair = lax.ppermute(features, "sec", pair_swap)
        own_c = lax.ppermute(features, "strip", core_swap)
        rim = lax.dynamic_slice_in_dim(features, 9 * core, 3, 1)
        edge = lax.dynamic_slice_in_dim(features, 3 * core, HALO, 1)
        third = arranged(w_third)
        pair, own_c, rim, edge, third = lax.optimization_barrier((pair, own_c, rim, edge, third))
        outer = lax.ppermute(pair, "sec", onward)
        far = jnp.concatenate([rim, lax.dynamic_slice_in_dim(pair, 3 * core, HALO, 1)], 1)
        far = lax.ppermute(far, "strip", chip_swap)
        outer_x = lax.ppermute(edge, both, next_chip)
        pair_c = lax.ppermute(
            lax.dynamic_slice_in_dim(pair, 3 * (1 - core), HALO, 1), "strip", core_swap
        )
        part, own_all, first, bias = pair_part(
            offsets, (features, far, own_c, pair, pair_c), w_first, b_first[None], b_second[None]
        )
        outer, part = lax.optimization_barrier((outer, part))
        near = lax.dynamic_slice_in_dim(outer, 3 * (1 - core), HALO, 1)
        outer_c = lax.ppermute(near, "strip", core_swap)
        out = align(
            offsets,
            part,
            own_all,
            (outer, outer_x, outer_c),
            (first, w_second, third),
            bias,
            state.reshape(2, STRIP, 1, LANES),
            strips * STRIP,
        )
        return out.reshape(2, 1, STRIP, LANES)

    return body


def solution(mesh):
    sections, strips = mesh.shape["sec"], mesh.shape["strip"]
    in_specs = (
        P("sec", "strip", None, None),
        P(),
        P(None, "sec", "strip", None),
        P(),
        P(),
        P(),
        P(),
        P(),
    )
    out_specs = P(None, "sec", "strip", None)
    return jax.shard_map(
        make_body(sections, strips), mesh=mesh, in_specs=in_specs, out_specs=out_specs, check_vma=False
    )
```

```python
import jax
import jax.numpy as jnp
from jax import lax
from jax.experimental import pallas as pl
from jax.experimental.pallas import tpu as pltpu
from jax.sharding import PartitionSpec as P

C = 128
STRIP = 12
HALO = 9
LANES = 128


def turned(nrot_ref, mid, far, near, core, shift, far_low, far_high, near_low):
    for k in range(26):
        at = k - 7 + shift
        row = mid[0, jnp.clip(at, 0, STRIP - 1)]
        if k < 9:
            low_far = far[0, jnp.clip(at + HALO, 0, HALO - 1) + far_low]
            low_near = near[0, jnp.clip(at + HALO, 0, HALO - 1) + near_low]
            row = jnp.where(at < 0, jnp.where(core == 0, low_far, low_near), row)
        if k > 16:
            high_far = far[0, jnp.clip(at - STRIP, 0, HALO - 1) + far_high]
            high_near = near[0, jnp.clip(at - STRIP, 0, HALO - 1)]
            row = jnp.where(at >= STRIP, jnp.where(core == 0, high_near, high_far), row)
        turn = 16 * (k % 8)
        if turn:
            nrot_ref[k, turn:] = row[: LANES - turn]
            nrot_ref[k, :turn] = row[LANES - turn :]
        else:
            nrot_ref[k] = row


def corr_rows(own_ref, corr_ref, nrot_ref, acc_ref, acc8_ref):
    col = lax.broadcasted_iota(jnp.int32, (LANES, LANES), 0)
    lane = lax.broadcasted_iota(jnp.int32, (LANES, LANES), 1)
    place = (lane - col + 4) & 127
    for k in range(0, 26, 2):
        first, last = max(0, k - 8), min(17, k + 1)
        right = nrot_ref[k : k + 2].reshape(2 * LANES, C)
        for i in range(first, last + 1):
            both = lax.dot_general(
                own_ref[i], right, (((1,), (1,)), ((), ())), preferred_element_type=jnp.float32
            )
            for side in range(2):
                a = k + side - i
                part = both[:, side * LANES : (side + 1) * LANES]
                if a == 8:
                    acc8_ref[i] = part
                elif 0 <= a < 8:
                    mask = (place >> 4) == (k + side) % 8
                    pltpu.store(acc_ref.at[i], part, mask=mask)
    step_row = (lane * 57) >> 9
    step_col = lane - 9 * step_row
    reach = col + step_col - 4
    valid = (reach >= 0) & (reach < LANES)
    start = 16 * step_row + reach
    for i in range(18):
        index = (start + 16 * i) & 127
        merged = jnp.take_along_axis(acc_ref[i], index, axis=1)
        last_a = jnp.take_along_axis(acc8_ref[i], index, axis=1)
        band = jnp.where(lane < 72, merged, last_a) * (C ** (-0.5))
        head = jnp.where(valid[:8], band[:8], 0.0)
        tail = jnp.where(valid[-8:], band[-8:], 0.0)
        corr_ref[i] = jnp.concatenate([head, band[8:-8], tail], axis=0).astype(jnp.bfloat16)


def shifted_sum(wide):
    row = lax.broadcasted_iota(jnp.int32, (8, C), 0)
    left = pltpu.roll(wide[:, :C], 1, 0)
    left = jnp.concatenate([jnp.where(row == 0, 0.0, left[:8]), left[8:]], axis=0)
    right = pltpu.roll(wide[:, 2 * C :], LANES - 1, 0)
    right = jnp.concatenate([right[:-8], jnp.where(row == 7, 0.0, right[-8:])], axis=0)
    return left + wide[:, C : 2 * C] + right


def position(off_ref):
    sec = lax.axis_index("sec")
    strip = lax.axis_index("strip")
    core = lax.rem(strip, 2)
    parity = lax.rem(sec, 2)
    above = off_ref[sec]
    below = jnp.where(sec > 0, -off_ref[jnp.maximum(sec - 1, 0)], 0)
    return core, parity, strip * STRIP, above, below


def convolved(rows, kernel_blocks, m):
    left = jnp.concatenate([rows[m + dy] for dy in range(4)], axis=1)
    both = jnp.dot(left, kernel_blocks, preferred_element_type=jnp.float32)
    return shifted_sum(both[:, : 3 * C]), shifted_sum(both[:, 3 * C :])


def blocks_of(w_ref):
    zeros = jnp.zeros((C, 3 * C), jnp.bfloat16)
    taps = [jnp.concatenate([w_ref[dy, dx] for dx in range(3)], axis=1) for dy in range(3)]
    low = jnp.concatenate(taps + [zeros], axis=0)
    return jnp.concatenate([low, jnp.concatenate([zeros] + taps, axis=0)], axis=1)


def pair_kernel(
    off_ref, own, far, own_c, pair, pair_c, w_ref, bias_ref, part_ref, own_buf, w_outer, bias_out,
    nrot_ref, acc_ref, acc8_ref, corr_ref, w_pair, halves,
):
    core, parity, top, above, below = position(off_ref)
    zeros = jnp.zeros((LANES, C), jnp.bfloat16)
    for dy in range(3):
        for dx in range(3):
            for half in range(2):
                halves[half] = zeros
                halves[half, :81] = w_ref[dy, dx, 81 * half : 81 * half + 81]
            w_pair[dy, dx] = halves[1 - parity]
            w_outer[dy, dx] = halves[parity]
    for r in range(3):
        own_buf[r] = jnp.where(core == 0, far[0, r], own_c[0, 9 + r])
        own_buf[15 + r] = jnp.where(core == 0, own_c[0, r], far[0, r])
    for r in range(STRIP):
        own_buf[3 + r] = own[0, r]
    shift = jnp.where(parity == 0, above, below)
    turned(nrot_ref, pair, far, pair_c, core, shift, 3, 3, 0)
    corr_rows(own_buf, corr_ref, nrot_ref, acc_ref, acc8_ref)
    bias_out[...] = bias_ref[1:2]
    kernel_blocks = blocks_of(w_pair)
    for m in range(0, 16, 2):
        for side, value in enumerate(convolved(corr_ref, kernel_blocks, m)):
            part_ref[m + side] = value + bias_ref[0:1]


def make_kernel(total_rows):
    def kernel(
        off_ref, part_ref, own_buf, outer, outer_x, outer_c, w1_ref, w2_ref, w3_ref, b2_ref,
        state_ref, out_ref, nrot_ref, acc_ref, acc8_ref, corr_ref, h1_ref, h2_ref, held_ref, sem,
    ):
        held = pltpu.make_async_copy(state_ref, held_ref, sem)
        held.start()
        core, parity, top, above, below = position(off_ref)
        shift = jnp.where(parity == 0, below, above)
        turned(nrot_ref, outer, outer_x, outer_c, core, shift, 0, 0, 0)
        corr_rows(own_buf, corr_ref, nrot_ref, acc_ref, acc8_ref)
        first = blocks_of(w1_ref)
        second = blocks_of(w2_ref)
        for m in range(0, 16, 2):
            for r, value in enumerate(convolved(corr_ref, first, m), m):
                value = jnp.maximum(part_ref[r] + value, 0.0)
                if r < 2 or r > 13:
                    row = top + (r - 2)
                    value = jnp.where((row >= 0) & (row < total_rows), value, 0.0)
                h1_ref[r] = value.astype(jnp.bfloat16)
        for n in range(0, 14, 2):
            for r, value in enumerate(convolved(h1_ref, second, n), n):
                value = jnp.maximum(value + b2_ref[...], 0.0)
                if r < 1 or r > 12:
                    row = top + (r - 1)
                    value = jnp.where((row >= 0) & (row < total_rows), value, 0.0)
                h2_ref[r] = value.astype(jnp.bfloat16)
        lane = lax.broadcasted_iota(jnp.int32, (8, LANES), 1)
        sums = []
        for n in range(0, 14, 2):
            taps = lax.dot_general(
                w3_ref[...],
                h2_ref[n : n + 2].reshape(2 * LANES, C),
                (((1,), (1,)), ((), ())),
                preferred_element_type=jnp.float32,
            )
            for side in range(2):
                tap = taps[:, side * LANES : (side + 1) * LANES]
                left = jnp.where(lane == 0, 0.0, pltpu.roll(tap[:8], 1, 1))
                right = jnp.where(lane == LANES - 1, 0.0, pltpu.roll(tap[16:], LANES - 1, 1))
                sums.append(left + tap[8:16] + right)
        held.wait()
        for r in range(12):
            delta = sums[r][0:2] + sums[r + 1][2:4] + sums[r + 2][4:6]
            out_ref[:, r, 0, :] = held_ref[:, r, 0, :] + delta

    return kernel


HBM = pl.BlockSpec(memory_space=pl.ANY)
VMEM = pl.BlockSpec(memory_space=pltpu.VMEM)
SMEM = pl.BlockSpec(memory_space=pltpu.SMEM)
PARAMS = pltpu.CompilerParams(vmem_limit_bytes=32 * 1024 * 1024)
CORR = [
    pltpu.VMEM((26, LANES, C), jnp.bfloat16),
    pltpu.VMEM((18, LANES, LANES), jnp.float32),
    pltpu.VMEM((18, LANES, LANES), jnp.float32),
    pltpu.VMEM((18, LANES, LANES), jnp.bfloat16),
]
TAPS = pltpu.VMEM((3, 3, LANES, C), jnp.bfloat16)


def pair_part(offsets, blocks, w_first, biases):
    return pl.pallas_call(
        pair_kernel,
        out_shape=(
            jax.ShapeDtypeStruct((16, LANES, C), jnp.float32),
            jax.ShapeDtypeStruct((18, LANES, C), jnp.bfloat16),
            jax.ShapeDtypeStruct((3, 3, LANES, C), jnp.bfloat16),
            jax.ShapeDtypeStruct((1, C), jnp.float32),
        ),
        in_specs=[SMEM] + [VMEM] * 7,
        out_specs=(VMEM, VMEM, VMEM, VMEM),
        scratch_shapes=CORR + [TAPS, pltpu.VMEM((2, LANES, C), jnp.bfloat16)],
        compiler_params=PARAMS,
        cost_estimate=pl.CostEstimate(
            flops=2 * 18 * 9 * LANES * LANES * C, bytes_accessed=100 * LANES * C * 2, transcendentals=0
        ),
    )(offsets, *blocks, w_first, biases)


def align(offsets, part, own, blocks, weights, b_second, state, total_rows):
    return pl.pallas_call(
        make_kernel(total_rows),
        out_shape=jax.ShapeDtypeStruct((2, STRIP, 1, LANES), jnp.float32),
        in_specs=[SMEM] + [VMEM] * 9 + [HBM],
        out_specs=VMEM,
        scratch_shapes=CORR
        + [
            pltpu.VMEM((16, LANES, C), jnp.bfloat16),
            pltpu.VMEM((14, LANES, C), jnp.bfloat16),
            pltpu.VMEM((2, STRIP, 1, LANES), jnp.float32),
            pltpu.SemaphoreType.DMA,
        ],
        compiler_params=PARAMS,
    )(offsets, part, own, *blocks, *weights, b_second, state)


def arranged(w_third):
    third = jnp.pad(w_third.transpose(1, 0, 3, 2).reshape(3, 6, 128), ((0, 0), (0, 2), (0, 0)))
    return third.reshape(24, 128)


def make_body(sections, strips):
    both = ("sec", "strip")
    core_swap = [(t, t ^ 1) for t in range(strips)]
    chip_swap = [(t, ((t + 1) ^ 1) - 1) for t in range(1, strips - 1)]
    pair_swap = [(s, s ^ 1) for s in range(sections)]
    onward = [(s, s + 2 if s % 2 == 0 else s - 2) for s in range(sections)]
    onward = [(s, d) for s, d in onward if 0 <= d < sections]
    next_chip = [(s ^ 1, d) for s, d in onward]
    next_chip = [(s * strips + t, d * strips + u) for s, d in next_chip for t, u in chip_swap]

    def body(features, offsets, state, w_first, b_first, w_second, b_second, w_third):
        core = lax.rem(lax.axis_index("strip"), 2)
        pair = lax.ppermute(features, "sec", pair_swap)
        own_c = lax.ppermute(features, "strip", core_swap)
        rim = lax.dynamic_slice_in_dim(features, 9 * core, 3, 1)
        edge = lax.dynamic_slice_in_dim(features, 3 * core, HALO, 1)
        third = arranged(w_third)
        offsets = jnp.clip(offsets, -2, 2)
        biases = jnp.stack([b_first, b_second])
        pair, own_c, rim, edge, third, offsets, biases = lax.optimization_barrier(
            (pair, own_c, rim, edge, third, offsets, biases)
        )
        outer = lax.ppermute(pair, "sec", onward)
        far = jnp.concatenate([rim, lax.dynamic_slice_in_dim(pair, 3 * core, HALO, 1)], 1)
        far = lax.ppermute(far, "strip", chip_swap)
        outer_x = lax.ppermute(edge, both, next_chip)
        pair_c = lax.ppermute(
            lax.dynamic_slice_in_dim(pair, 3 * (1 - core), HALO, 1), "strip", core_swap
        )
        part, own_all, first, bias = pair_part(
            offsets, (features, far, own_c, pair, pair_c), w_first, biases
        )
        outer, part = lax.optimization_barrier((outer, part))
        near = lax.dynamic_slice_in_dim(outer, 3 * (1 - core), HALO, 1)
        outer_c = lax.ppermute(near, "strip", core_swap)
        out = align(
            offsets,
            part,
            own_all,
            (outer, outer_x, outer_c),
            (first, w_second, third),
            bias,
            state.reshape(2, STRIP, 1, LANES),
            strips * STRIP,
        )
        return out.reshape(2, 1, STRIP, LANES)

    return body


def solution(mesh):
    sections, strips = mesh.shape["sec"], mesh.shape["strip"]
    in_specs = (
        P("sec", "strip", None, None),
        P(),
        P(None, "sec", "strip", None),
        P(),
        P(),
        P(),
        P(),
        P(),
    )
    out_specs = P(None, "sec", "strip", None)
    return jax.shard_map(
        make_body(sections, strips), mesh=mesh, in_specs=in_specs, out_specs=out_specs, check_vma=False
    )
```

```python
import jax
import jax.numpy as jnp
from jax import lax
from jax.experimental import pallas as pl
from jax.experimental.pallas import tpu as pltpu
from jax.sharding import PartitionSpec as P

C = 128
STRIP = 12
HALO = 9
LANES = 128


def turned(nrot_ref, mid, far, near, core, shift, far_low, far_high, near_low):
    for k in range(26):
        at = k - 7 + shift
        row = mid[0, jnp.clip(at, 0, STRIP - 1)]
        if k < 9:
            low_far = far[0, jnp.clip(at + HALO, 0, HALO - 1) + far_low]
            low_near = near[0, jnp.clip(at + HALO, 0, HALO - 1) + near_low]
            row = jnp.where(at < 0, jnp.where(core == 0, low_far, low_near), row)
        if k > 16:
            high_far = far[0, jnp.clip(at - STRIP, 0, HALO - 1) + far_high]
            high_near = near[0, jnp.clip(at - STRIP, 0, HALO - 1)]
            row = jnp.where(at >= STRIP, jnp.where(core == 0, high_near, high_far), row)
        turn = 16 * (k % 8)
        if turn:
            nrot_ref[k, turn:] = row[: LANES - turn]
            nrot_ref[k, :turn] = row[LANES - turn :]
        else:
            nrot_ref[k] = row


def corr_rows(own_ref, corr_ref, nrot_ref, acc_ref, acc8_ref):
    col = lax.broadcasted_iota(jnp.int32, (LANES, LANES), 0)
    lane = lax.broadcasted_iota(jnp.int32, (LANES, LANES), 1)
    place = (lane - col + 4) & 127
    for k in range(0, 26, 2):
        first, last = max(0, k - 8), min(17, k + 1)
        right = nrot_ref[k : k + 2].reshape(2 * LANES, C)
        for i in range(first, last + 1):
            both = lax.dot_general(
                own_ref[i], right, (((1,), (1,)), ((), ())), preferred_element_type=jnp.float32
            )
            for side in range(2):
                a = k + side - i
                part = both[:, side * LANES : (side + 1) * LANES]
                if a == 8:
                    acc8_ref[i] = part
                elif 0 <= a < 8:
                    mask = (place >> 4) == (k + side) % 8
                    pltpu.store(acc_ref.at[i], part, mask=mask)
    step_row = (lane * 57) >> 9
    step_col = lane - 9 * step_row
    reach = col + step_col - 4
    valid = (reach >= 0) & (reach < LANES)
    start = 16 * step_row + reach
    for i in range(18):
        index = (start + 16 * i) & 127
        merged = jnp.take_along_axis(acc_ref[i], index, axis=1)
        last_a = jnp.take_along_axis(acc8_ref[i], index, axis=1)
        band = jnp.where(lane < 72, merged, last_a) * (C ** (-0.5))
        head = jnp.where(valid[:8], band[:8], 0.0)
        tail = jnp.where(valid[-8:], band[-8:], 0.0)
        corr_ref[i] = jnp.concatenate([head, band[8:-8], tail], axis=0).astype(jnp.bfloat16)


def shifted_sum(wide):
    row = lax.broadcasted_iota(jnp.int32, (8, C), 0)
    left = pltpu.roll(wide[:, :C], 1, 0)
    left = jnp.concatenate([jnp.where(row == 0, 0.0, left[:8]), left[8:]], axis=0)
    right = pltpu.roll(wide[:, 2 * C :], LANES - 1, 0)
    right = jnp.concatenate([right[:-8], jnp.where(row == 7, 0.0, right[-8:])], axis=0)
    return left + wide[:, C : 2 * C] + right


def position(off_ref):
    sec = lax.axis_index("sec")
    strip = lax.axis_index("strip")
    core = lax.rem(strip, 2)
    parity = lax.rem(sec, 2)
    above = off_ref[sec]
    below = jnp.where(sec > 0, -off_ref[jnp.maximum(sec - 1, 0)], 0)
    return core, parity, strip * STRIP, above, below


def convolved(rows, kernel_blocks, m):
    left = jnp.concatenate([rows[m + dy] for dy in range(4)], axis=1)
    both = jnp.dot(left, kernel_blocks, preferred_element_type=jnp.float32)
    return shifted_sum(both[:, : 3 * C]), shifted_sum(both[:, 3 * C :])


def blocks_of(w_ref):
    zeros = jnp.zeros((C, 3 * C), jnp.bfloat16)
    taps = [jnp.concatenate([w_ref[dy, dx] for dx in range(3)], axis=1) for dy in range(3)]
    low = jnp.concatenate(taps + [zeros], axis=0)
    return jnp.concatenate([low, jnp.concatenate([zeros] + taps, axis=0)], axis=1)


def pair_kernel(
    off_ref, own, far, own_c, pair, pair_c, w_ref, bias_ref, part_ref, own_buf, w_outer, bias_out,
    nrot_ref, acc_ref, acc8_ref, corr_ref, w_pair, halves,
):
    core, parity, top, above, below = position(off_ref)
    zeros = jnp.zeros((LANES, C), jnp.bfloat16)
    for dy in range(3):
        for dx in range(3):
            for half in range(2):
                halves[half] = zeros
                halves[half, :81] = w_ref[dy, dx, 81 * half : 81 * half + 81]
            w_pair[dy, dx] = halves[1 - parity]
            w_outer[dy, dx] = halves[parity]
    for r in range(3):
        own_buf[r] = jnp.where(core == 0, far[0, r], own_c[0, r])
        own_buf[15 + r] = jnp.where(core == 0, own_c[0, r], far[0, r])
    for r in range(STRIP):
        own_buf[3 + r] = own[0, r]
    shift = jnp.where(parity == 0, above, below)
    turned(nrot_ref, pair, far, pair_c, core, shift, 3, 3, 0)
    corr_rows(own_buf, corr_ref, nrot_ref, acc_ref, acc8_ref)
    bias_out[...] = bias_ref[1:2]
    kernel_blocks = blocks_of(w_pair)
    for m in range(0, 16, 2):
        for side, value in enumerate(convolved(corr_ref, kernel_blocks, m)):
            part_ref[m + side] = value + bias_ref[0:1]


def make_kernel(total_rows):
    def kernel(
        off_ref, part_ref, own_buf, outer, outer_x, outer_c, w1_ref, w2_ref, w3_ref, b2_ref,
        state_ref, out_ref, nrot_ref, acc_ref, acc8_ref, corr_ref, h1_ref, h2_ref, held_ref, sem,
    ):
        held = pltpu.make_async_copy(state_ref, held_ref, sem)
        held.start()
        core, parity, top, above, below = position(off_ref)
        shift = jnp.where(parity == 0, below, above)
        turned(nrot_ref, outer, outer_x, outer_c, core, shift, 0, 0, 0)
        corr_rows(own_buf, corr_ref, nrot_ref, acc_ref, acc8_ref)
        first = blocks_of(w1_ref)
        second = blocks_of(w2_ref)
        for m in range(0, 16, 2):
            for r, value in enumerate(convolved(corr_ref, first, m), m):
                value = jnp.maximum(part_ref[r] + value, 0.0)
                if r < 2 or r > 13:
                    row = top + (r - 2)
                    value = jnp.where((row >= 0) & (row < total_rows), value, 0.0)
                h1_ref[r] = value.astype(jnp.bfloat16)
        for n in range(0, 14, 2):
            for r, value in enumerate(convolved(h1_ref, second, n), n):
                value = jnp.maximum(value + b2_ref[...], 0.0)
                if r < 1 or r > 12:
                    row = top + (r - 1)
                    value = jnp.where((row >= 0) & (row < total_rows), value, 0.0)
                h2_ref[r] = value.astype(jnp.bfloat16)
        lane = lax.broadcasted_iota(jnp.int32, (8, LANES), 1)
        sums = []
        for n in range(0, 14, 2):
            taps = lax.dot_general(
                w3_ref[...],
                h2_ref[n : n + 2].reshape(2 * LANES, C),
                (((1,), (1,)), ((), ())),
                preferred_element_type=jnp.float32,
            )
            for side in range(2):
                tap = taps[:, side * LANES : (side + 1) * LANES]
                left = jnp.where(lane == 0, 0.0, pltpu.roll(tap[:8], 1, 1))
                right = jnp.where(lane == LANES - 1, 0.0, pltpu.roll(tap[16:], LANES - 1, 1))
                sums.append(left + tap[8:16] + right)
        held.wait()
        for r in range(12):
            delta = sums[r][0:2] + sums[r + 1][2:4] + sums[r + 2][4:6]
            out_ref[:, r, 0, :] = held_ref[:, r, 0, :] + delta

    return kernel


HBM = pl.BlockSpec(memory_space=pl.ANY)
VMEM = pl.BlockSpec(memory_space=pltpu.VMEM)
SMEM = pl.BlockSpec(memory_space=pltpu.SMEM)
PARAMS = pltpu.CompilerParams(vmem_limit_bytes=32 * 1024 * 1024)
CORR = [
    pltpu.VMEM((26, LANES, C), jnp.bfloat16),
    pltpu.VMEM((18, LANES, LANES), jnp.float32),
    pltpu.VMEM((18, LANES, LANES), jnp.float32),
    pltpu.VMEM((18, LANES, LANES), jnp.bfloat16),
]
TAPS = pltpu.VMEM((3, 3, LANES, C), jnp.bfloat16)


def pair_part(offsets, blocks, w_first, biases):
    return pl.pallas_call(
        pair_kernel,
        out_shape=(
            jax.ShapeDtypeStruct((16, LANES, C), jnp.float32),
            jax.ShapeDtypeStruct((18, LANES, C), jnp.bfloat16),
            jax.ShapeDtypeStruct((3, 3, LANES, C), jnp.bfloat16),
            jax.ShapeDtypeStruct((1, C), jnp.float32),
        ),
        in_specs=[SMEM] + [VMEM] * 7,
        out_specs=(VMEM, VMEM, VMEM, VMEM),
        scratch_shapes=CORR + [TAPS, pltpu.VMEM((2, LANES, C), jnp.bfloat16)],
        compiler_params=PARAMS,
        cost_estimate=pl.CostEstimate(
            flops=2 * 18 * 9 * LANES * LANES * C, bytes_accessed=100 * LANES * C * 2, transcendentals=0
        ),
    )(offsets, *blocks, w_first, biases)


def align(offsets, part, own, blocks, weights, b_second, state, total_rows):
    return pl.pallas_call(
        make_kernel(total_rows),
        out_shape=jax.ShapeDtypeStruct((2, STRIP, 1, LANES), jnp.float32),
        in_specs=[SMEM] + [VMEM] * 9 + [HBM],
        out_specs=VMEM,
        scratch_shapes=CORR
        + [
            pltpu.VMEM((16, LANES, C), jnp.bfloat16),
            pltpu.VMEM((14, LANES, C), jnp.bfloat16),
            pltpu.VMEM((2, STRIP, 1, LANES), jnp.float32),
            pltpu.SemaphoreType.DMA,
        ],
        compiler_params=PARAMS,
    )(offsets, part, own, *blocks, *weights, b_second, state)


def arranged(w_third):
    third = jnp.pad(w_third.transpose(1, 0, 3, 2).reshape(3, 6, 128), ((0, 0), (0, 2), (0, 0)))
    return third.reshape(24, 128)


def make_body(sections, strips):
    both = ("sec", "strip")
    core_swap = [(t, t ^ 1) for t in range(strips)]
    chip_swap = [(t, ((t + 1) ^ 1) - 1) for t in range(1, strips - 1)]
    pair_swap = [(s, s ^ 1) for s in range(sections)]
    onward = [(s, s + 2 if s % 2 == 0 else s - 2) for s in range(sections)]
    onward = [(s, d) for s, d in onward if 0 <= d < sections]
    next_chip = [(s ^ 1, d) for s, d in onward]
    next_chip = [(s * strips + t, d * strips + u) for s, d in next_chip for t, u in chip_swap]

    def body(features, offsets, state, w_first, b_first, w_second, b_second, w_third):
        core = lax.rem(lax.axis_index("strip"), 2)
        pair = lax.ppermute(features, "sec", pair_swap)
        own_c = lax.ppermute(
            lax.dynamic_slice_in_dim(features, 9 * (1 - core), 3, 1), "strip", core_swap
        )
        rim = lax.dynamic_slice_in_dim(features, 9 * core, 3, 1)
        edge = lax.dynamic_slice_in_dim(features, 3 * core, HALO, 1)
        third = arranged(w_third)
        offsets = jnp.clip(offsets, -2, 2)
        biases = jnp.stack([b_first, b_second])
        pair, own_c, rim, edge, third, offsets, biases = lax.optimization_barrier(
            (pair, own_c, rim, edge, third, offsets, biases)
        )
        outer = lax.ppermute(pair, "sec", onward)
        far = jnp.concatenate([rim, lax.dynamic_slice_in_dim(pair, 3 * core, HALO, 1)], 1)
        far = lax.ppermute(far, "strip", chip_swap)
        outer_x = lax.ppermute(edge, both, next_chip)
        pair_c = lax.ppermute(
            lax.dynamic_slice_in_dim(pair, 3 * (1 - core), HALO, 1), "strip", core_swap
        )
        part, own_all, first, bias = pair_part(
            offsets, (features, far, own_c, pair, pair_c), w_first, biases
        )
        outer, part = lax.optimization_barrier((outer, part))
        near = lax.dynamic_slice_in_dim(outer, 3 * (1 - core), HALO, 1)
        outer_c = lax.ppermute(near, "strip", core_swap)
        out = align(
            offsets,
            part,
            own_all,
            (outer, outer_x, outer_c),
            (first, w_second, third),
            bias,
            state.reshape(2, STRIP, 1, LANES),
            strips * STRIP,
        )
        return out.reshape(2, 1, STRIP, LANES)

    return body


def solution(mesh):
    sections, strips = mesh.shape["sec"], mesh.shape["strip"]
    in_specs = (
        P("sec", "strip", None, None),
        P(),
        P(None, "sec", "strip", None),
        P(),
        P(),
        P(),
        P(),
        P(),
    )
    out_specs = P(None, "sec", "strip", None)
    return jax.shard_map(
        make_body(sections, strips), mesh=mesh, in_specs=in_specs, out_specs=out_specs, check_vma=False
    )
```
